32 devices in a mesh: shard: 2 (over x), ctx: 4 (over y, core), tensor: 4 (over z).
Axes of the slice: x: 2, y: 2, z: 4, core: 2. Of those that a mesh axis runs over, the one named last changes fastest.
Arguments:
- hidden: bfloat16 [4, 1024, 1024], P('shard', 'ctx'), may hold values from -6 to 6
- out_grad: bfloat16 [4, 1024, 1024], P('shard', 'ctx'), may hold values from -6 to 6
- norm_gain: float32 [1024], replicated, may hold values from 0.5 to 1.5
- mlp_gain: float32 [1024], replicated, may hold values from 0.5 to 1.5
- in_proj: bfloat16 [1024, 2, 1536], P(('shard', 'ctx'), None, 'tensor'), may hold values from -0.1875 to 0.1875
- step_proj: bfloat16 [1024, 24], P(('shard', 'ctx'), 'tensor'), may hold values from -0.1875 to 0.1875
- bc_proj: bfloat16 [1024, 256], P(('shard', 'ctx')), may hold values from -0.1875 to 0.1875
- out_proj: bfloat16 [1536, 1024], P('tensor', ('shard', 'ctx')), may hold values from -0.15625 to 0.15625
- q_proj: bfloat16 [1024, 1024], P(('shard', 'ctx'), 'tensor'), may hold values from -0.5 to 0.5
- kv_proj: bfloat16 [1024, 2, 2, 128], P(('shard', 'ctx')), may hold values from -0.5 to 0.5
- o_proj: bfloat16 [1024, 1024], P('tensor', ('shard', 'ctx')), may hold values from -0.5 to 0.5
- gate_up: bfloat16 [1024, 2, 2048], P(('shard', 'ctx'), None, 'tensor'), may hold values from -0.1875 to 0.1875
- down_proj: bfloat16 [2048, 1024], P('tensor', ('shard', 'ctx')), may hold values from -0.125 to 0.125
- conv_weight: float32 [4, 1792], replicated, may hold values from -3 to 3
- conv_bias: float32 [1792], replicated, may hold values from -0.5 to 0.5
- log_rate: float32 [24], replicated, may hold values from 0 to 2.5
- step_bias: float32 [24], replicated, may hold values from -6 to -2
- skip_gain: float32 [24], replicated, may hold values from 0.5 to 1.5
- gate_gain: float32 [1536], replicated, may hold values from 0.5 to 1.5
Outputs:
- output: bfloat16 [4, 1024, 1024], P('shard', 'ctx')
- d_hidden: float32 [4, 1024, 1024], P('shard', 'ctx')
- grad_norm_gain: float32 [1024], replicated
- grad_mlp_gain: float32 [1024], replicated
- grad_in_proj: float32 [1024, 2, 1536], P(('shard', 'ctx'), None, 'tensor')
- grad_step_proj: float32 [1024, 24], P(('shard', 'ctx'), 'tensor')
- grad_bc_proj: float32 [1024, 256], P(('shard', 'ctx', 'tensor'))
- grad_out_proj: float32 [1536, 1024], P('tensor', ('shard', 'ctx'))
- grad_q_proj: float32 [1024, 1024], P(('shard', 'ctx'), 'tensor')
- grad_kv_proj: float32 [1024, 2, 2, 128], P(('shard', 'ctx', 'tensor'))
- grad_o_proj: float32 [1024, 1024], P('tensor', ('shard', 'ctx'))
- grad_gate_up: float32 [1024, 2, 2048], P(('shard', 'ctx'), None, 'tensor')
- grad_down_proj: float32 [2048, 1024], P('tensor', ('shard', 'ctx'))
- grad_conv_weight: float32 [4, 1792], replicated
- grad_conv_bias: float32 [1792], replicated
- grad_log_rate: float32 [24], replicated
- grad_step_bias: float32 [24], replicated
- grad_skip_gain: float32 [24], replicated
- grad_gate_gain: float32 [1536], replicated
The draws below stay inside these ranges and needn't reach their ends.
All inputs are finite; a program needn't handle non-finite values.
Results may differ from the reference program's by a relative error of at most 0.02.
Values may be sent and summed in bfloat16 or wider, within the bound.
No kernel may reach another device: no remote copies, remote signals or barrier semaphores. Data moves between devices by JAX's collectives and lax.ppermute only.
A program may use at most 128 MiB of HBM per device.

```python
import math
import jax
import jax.numpy as jnp
from jax import lax

D = 1024
FF = 2048
MH = 24
HDM = 64
NSTATE = 128
CONV = 4
AH = 8
KVH = 2
HD = 128
GN_GROUP = 384
LC = 256
DI = 1536
CH = 1792
LEN = 1024
SEQS = 4
N_CTX = 4
N_TENSOR = 4


def draw_hidden(key, part):
    values = jax.random.truncated_normal(jax.random.fold_in(key, 31), -6.0, 6.0, (SEQS, LEN, D), jnp.float32)
    return values.astype(jnp.bfloat16)


def draw_q_proj(key, part):
    scale_d = 1.0 / math.sqrt(D)
    entries = jax.random.truncated_normal(jax.random.fold_in(key, 41), -4.0, 4.0, (D, AH, HD), jnp.float32) * scale_d
    return entries.reshape(D, AH * HD).astype(jnp.bfloat16)


def draw_kv_proj(key, part):
    scale_d = 1.0 / math.sqrt(D)
    entries = jax.random.truncated_normal(jax.random.fold_in(key, 53), -4.0, 4.0, (D, KVH, 2, HD), jnp.float32) * scale_d
    return entries.astype(jnp.bfloat16)


def shard_levels(rng, extent, cuts, smallest, largest):
    factor_of, own = 1.0, jax.random.fold_in(rng, 6)
    for dim, parts in cuts:
        steps = jnp.exp(jax.random.uniform(jax.random.fold_in(own, dim), (parts,), jnp.float32, smallest / len(cuts), largest / len(cuts)))
        factor_of = factor_of * jnp.repeat(steps, extent[dim] // parts).reshape([-1 if axis == dim else 1 for axis in range(len(extent))])
    return factor_of


def bell_draw(rng, extent, deviation, reach, cuts=(), kind=jnp.bfloat16):
    values = deviation * jax.random.normal(rng, extent, jnp.float32)
    if cuts:
        values = values * shard_levels(rng, extent, cuts, -0.22, 0.18)
    return jnp.clip(values, -reach, reach).astype(kind)


def setup_inputs(seed: int = 0) -> dict:
    keys = jax.random.split(jax.random.key(seed), 20)
    hidden = draw_hidden(jax.random.fold_in(keys[19], 71), 0)
    out_grad = bell_draw(keys[1], (SEQS, LEN, D), 1.0, 6.0, ((0, 2), (1, 4)))
    norm_gain = jnp.clip(1.0 + 0.1 * jax.random.normal(keys[2], (D,), jnp.float32), 0.5, 1.5)
    mlp_gain = jnp.clip(1.0 + 0.1 * jax.random.normal(keys[3], (D,), jnp.float32), 0.5, 1.5)
    in_proj = bell_draw(keys[4], (D, 2, DI), D ** -0.5, 0.1875, ((0, 8), (2, 4)))
    step_proj = bell_draw(keys[5], (D, MH), D ** -0.5, 0.1875, ((0, 8), (1, 4)))
    bc_proj = bell_draw(keys[6], (D, 2 * NSTATE), D ** -0.5, 0.1875, ((0, 8),))
    out_proj = bell_draw(keys[7], (DI, D), DI ** -0.5, 0.15625, ((0, 4), (1, 8)))
    q_proj = draw_q_proj(jax.random.fold_in(keys[19], 71), 0)
    kv_proj = draw_kv_proj(jax.random.fold_in(keys[19], 71), 0)
    o_proj = bell_draw(keys[10], (AH * HD, D), HD ** -0.5, 0.5, ((0, 4), (1, 8)))
    gate_up = bell_draw(keys[11], (D, 2, FF), D ** -0.5, 0.1875, ((0, 8), (2, 4)))
    down_proj = bell_draw(keys[12], (FF, D), FF ** -0.5, 0.125, ((0, 4), (1, 8)))
    conv_weight = bell_draw(keys[13], (CONV, CH), CONV ** -0.5, 3.0, (), jnp.float32)
    conv_bias = jnp.clip(jax.random.uniform(keys[14], (CH,), jnp.float32, -0.5, 0.5), -0.5, 0.5)
    log_rate = jnp.clip(jax.random.uniform(keys[15], (MH,), jnp.float32, 0.0, 2.5), 0.0, 2.5)
    step_bias = jnp.clip(jax.random.uniform(keys[16], (MH,), jnp.float32, -6.0, -2.0), -6.0, -2.0)
    skip_gain = jnp.clip(jax.random.uniform(keys[17], (MH,), jnp.float32, 0.5, 1.5), 0.5, 1.5)
    gate_gain = jnp.clip(1.0 + 0.1 * jax.random.normal(keys[18], (DI,), jnp.float32), 0.5, 1.5)
    return {"hidden": hidden, "out_grad": out_grad, "norm_gain": norm_gain, "mlp_gain": mlp_gain, "in_proj": in_proj, "step_proj": step_proj, "bc_proj": bc_proj, "out_proj": out_proj, "q_proj": q_proj, "kv_proj": kv_proj, "o_proj": o_proj, "gate_up": gate_up, "down_proj": down_proj, "conv_weight": conv_weight, "conv_bias": conv_bias, "log_rate": log_rate, "step_bias": step_bias, "skip_gain": skip_gain, "gate_gain": gate_gain}


EPS = 1e-05
ROPE_BASE = 100000000000.0
HIGHEST = lax.Precision.HIGHEST

def contract(form, left, right):
    return jnp.einsum(form, left.astype(jnp.float32), right.astype(jnp.float32))

def rms_forward(values, gain_vec):
    rms_scale = lax.rsqrt(lax.optimization_barrier(jnp.mean(values * values, axis=-1, keepdims=True)) + EPS)
    return (values * rms_scale * gain_vec, rms_scale)

def rms_backward(values, rms_scale, gain_vec, upstream):
    weighted = upstream * gain_vec
    inner_mean = lax.optimization_barrier(jnp.mean(weighted * values, axis=-1, keepdims=True))
    d_values = rms_scale * (weighted - values * rms_scale * rms_scale * inner_mean)
    d_gain = lax.optimization_barrier(jnp.sum((upstream * values * rms_scale).reshape(-1, values.shape[-1]), axis=0))
    return (d_values, d_gain)

def rope_tables(positions, vec_width):
    half_width = vec_width // 2
    inv_freq = jnp.exp(jnp.arange(half_width, dtype=jnp.float32) * (-2.0 * math.log(ROPE_BASE) / vec_width))
    rope_angle = positions.astype(jnp.float32)[:, None] * inv_freq[None, :]
    return (jnp.cos(rope_angle), jnp.sin(rope_angle))

def rotate(values, cosine, sine_tab, turn_sign):
    half_width = values.shape[-1] // 2
    first_half = values[..., :half_width]
    second = values[..., half_width:]
    cos_b = cosine[:, None, :]
    sin_b = turn_sign * sine_tab[:, None, :]
    return jnp.concatenate([first_half * cos_b - second * sin_b, second * cos_b + first_half * sin_b], axis=-1)

def conv_silu(extended, weight, bias_vec):
    tok_rows = extended.shape[-2] - weight.shape[0] + 1
    conv_sum = bias_vec + weight[0] * extended[..., 0:tok_rows, :]
    for conv_lag in range(1, weight.shape[0]):
        conv_sum = conv_sum + weight[conv_lag] * extended[..., conv_lag:conv_lag + tok_rows, :]
    return jax.nn.silu(conv_sum)

def decay_terms(raw_step, log_rates, step_shift):
    step_size = jax.nn.softplus(raw_step + step_shift)
    return (step_size, jnp.cumsum(step_size * -jnp.exp(log_rates), axis=1))

def ssd_output(inputs, b_mat, c_mat, raw_step, log_rates, step_shift, skip_vec, state_in):
    step_size, cum_rate = decay_terms(raw_step, log_rates, step_shift)
    tok_rows = cum_rate.shape[1]
    causal = jnp.arange(tok_rows)[:, None] >= jnp.arange(tok_rows)[None, :]
    heads_first = jnp.swapaxes(cum_rate, 1, 2)
    rate_gap = heads_first[:, :, :, None] - heads_first[:, :, None, :]
    kernel = jnp.where(causal, jnp.exp(jnp.where(causal, rate_gap, 0.0)), 0.0)
    inner_prod = jnp.einsum('bpn,bqn->bpq', c_mat, b_mat, precision=HIGHEST)
    kernel = kernel * inner_prod[:, None] * jnp.swapaxes(step_size, 1, 2)[:, :, None, :]
    local_part = jnp.einsum('bhpq,bqhd->bphd', kernel, inputs, precision=HIGHEST)
    carried = jnp.einsum('bpn,bhdn->bphd', c_mat, state_in, precision=HIGHEST) * jnp.exp(cum_rate)[..., None]
    return local_part + carried + skip_vec[..., None] * inputs

def state_terms(inputs, b_mat, raw_step, log_rates, step_shift):
    step_size, cum_rate = decay_terms(raw_step, log_rates, step_shift)
    last_rate = cum_rate[:, -1:, :]
    factor = jnp.exp(last_rate - cum_rate) * step_size
    local_part = jnp.einsum('bqh,bqhd,bqn->bhdn', factor, inputs, b_mat, precision=HIGHEST)
    return (jnp.exp(last_rate[:, 0, :]), local_part)

def gated_norm(mixed_y, gate_z, gain_vec):
    gated_y = mixed_y * jax.nn.silu(gate_z)
    grouped = gated_y.reshape(gated_y.shape[:-1] + (gated_y.shape[-1] // GN_GROUP, GN_GROUP))
    rms_scale = lax.rsqrt(lax.optimization_barrier(jnp.mean(grouped * grouped, axis=-1, keepdims=True)) + EPS)
    return (grouped * rms_scale).reshape(gated_y.shape) * gain_vec

def mamba_piece(z_and_x, bc_rep, raw_step, conv_w, conv_b, log_rates, step_shift, skip_vec, gain_vec):
    lags = conv_w.shape[0]
    heads_dev = MH // N_TENSOR
    x_ext = jnp.concatenate([jnp.zeros((lags - 1, DI), jnp.float32), z_and_x[:, 1]], axis=0)
    x_act = conv_silu(x_ext, conv_w[:, :DI], conv_b[:DI])
    bc_ext = jnp.concatenate([jnp.zeros((N_TENSOR, lags - 1, 2 * NSTATE), jnp.float32), bc_rep], axis=1)
    bc_act = conv_silu(bc_ext, conv_w[:, DI:], conv_b[DI:])
    x_blocks = x_act.reshape(N_CTX, LC, N_TENSOR, heads_dev, HDM).transpose(0, 2, 1, 3, 4)
    b_blocks = bc_act[:, :, :NSTATE].reshape(N_TENSOR, N_CTX, LC, NSTATE).transpose(1, 0, 2, 3)
    c_blocks = bc_act[:, :, NSTATE:].reshape(N_TENSOR, N_CTX, LC, NSTATE).transpose(1, 0, 2, 3)
    raw_blocks = raw_step.reshape(N_CTX, LC, N_TENSOR, heads_dev).transpose(0, 2, 1, 3)
    rate_blocks = log_rates.reshape(N_TENSOR, 1, heads_dev)
    shift_blocks = step_shift.reshape(N_TENSOR, 1, heads_dev)
    skip_blocks = skip_vec.reshape(N_TENSOR, 1, heads_dev)

    def stretch_step(state_now, pieces):
        x_part, b_part, c_part, raw_part = pieces
        y_part = ssd_output(x_part, b_part, c_part, raw_part, rate_blocks, shift_blocks, skip_blocks, state_now)
        decays, local_part = state_terms(x_part, b_part, raw_part, rate_blocks, shift_blocks)
        return (decays[:, :, None, None] * state_now + local_part, y_part)
    start_state = jnp.zeros((N_TENSOR, heads_dev, HDM, NSTATE), jnp.float32)
    final_state, y_parts = lax.scan(stretch_step, start_state, (x_blocks, b_blocks, c_blocks, raw_blocks))
    ssd_y = y_parts.transpose(0, 2, 1, 3, 4).reshape(LEN, DI)
    return gated_norm(ssd_y, z_and_x[:, 0], gain_vec)

def reference(hidden, out_grad, norm_gain, mlp_gain, in_proj, step_proj, bc_proj, out_proj, q_proj, kv_proj, o_proj, gate_up, down_proj, conv_weight, conv_bias, log_rate, step_bias, skip_gain, gate_gain):
    group_q = AH // KVH
    heads_dev = AH // N_TENSOR
    select = (jnp.arange(N_TENSOR)[:, None] * heads_dev // group_q == jnp.arange(KVH)[None, :]).astype(jnp.float32)
    positions = jnp.arange(LEN, dtype=jnp.int32)
    cosine, sine_tab = rope_tables(positions, HD)
    allowed = positions[None, :] <= positions[:, None]
    score_scale = 1.0 / math.sqrt(HD)
    params = (norm_gain, mlp_gain, in_proj, step_proj, bc_proj, out_proj, q_proj, kv_proj, o_proj, gate_up, down_proj, conv_weight, conv_bias, log_rate, step_bias, skip_gain, gate_gain)
    zero_sums = tuple((jnp.zeros(param.shape, jnp.float32) for param in params))

    def one_sequence(grad_sums, pieces):
        hid_bf, cotangent = pieces
        inputs32 = hid_bf.astype(jnp.float32)
        normed32, scale_one = rms_forward(inputs32, norm_gain)
        normed = normed32.astype(jnp.bfloat16)
        z_and_x = contract('pd,dkc->pkc', normed, in_proj)
        bc_pre = contract('pd,dn->pn', normed, bc_proj)
        raw_step = contract('pd,dh->ph', normed, step_proj)
        bc_rep = jnp.broadcast_to(bc_pre[None], (N_TENSOR,) + bc_pre.shape)
        mamba_f32, mamba_pull = jax.vjp(mamba_piece, z_and_x, bc_rep, raw_step, conv_weight, conv_bias, log_rate, step_bias, skip_gain, gate_gain)
        mamba_y = mamba_f32.astype(jnp.bfloat16)
        query_raw = contract('pd,dc->pc', normed, q_proj).reshape(LEN, AH, HD)
        kv_raw = contract('pd,dhkc->phkc', normed, kv_proj)
        queries = rotate(query_raw, cosine, sine_tab, 1.0).astype(jnp.bfloat16)
        key_rows = rotate(kv_raw[:, :, 0], cosine, sine_tab, 1.0).astype(jnp.bfloat16)
        value_rows = kv_raw[:, :, 1].astype(jnp.bfloat16)
        key_heads = jnp.repeat(key_rows, group_q, axis=1)
        value_heads = jnp.repeat(value_rows, group_q, axis=1)
        scores = contract('phc,khc->hpk', queries, key_heads) * score_scale
        scores = jnp.where(allowed, scores, -1e+30)
        row_peak = lax.optimization_barrier(jnp.max(scores, axis=-1, keepdims=True))
        log_total = row_peak + jnp.log(lax.optimization_barrier(jnp.sum(jnp.exp(scores - row_peak), axis=-1, keepdims=True)))
        attn_probs = jnp.exp(scores - log_total)
        probs_b = attn_probs.astype(jnp.bfloat16)
        attended = contract('hpk,khc->phc', probs_b, value_heads).astype(jnp.bfloat16)
        attended_flat = attended.reshape(LEN, AH * HD)
        mamba_parts = contract('pjc,jcd->jpd', mamba_y.reshape(LEN, N_TENSOR, DI // N_TENSOR), out_proj.reshape(N_TENSOR, DI // N_TENSOR, D))
        attn_parts = contract('pjc,jcd->jpd', attended_flat.reshape(LEN, N_TENSOR, heads_dev * HD), o_proj.reshape(N_TENSOR, heads_dev * HD, D))
        part_b = lax.optimization_barrier((mamba_parts + attn_parts).astype(jnp.bfloat16))
        mixed_sum = lax.optimization_barrier(jnp.sum(part_b.astype(jnp.float32), axis=0))
        middle = inputs32 + mixed_sum
        normed_two32, scale_two = rms_forward(middle, mlp_gain)
        normed_two = normed_two32.astype(jnp.bfloat16)
        gate_up32 = contract('pd,dkf->pkf', normed_two, gate_up)
        gate_pre = gate_up32[:, 0]
        up_pre = gate_up32[:, 1]
        swiglu = (jax.nn.silu(gate_pre) * up_pre).astype(jnp.bfloat16)
        mlp_parts = contract('pjf,jfd->jpd', swiglu.reshape(LEN, N_TENSOR, FF // N_TENSOR), down_proj.reshape(N_TENSOR, FF // N_TENSOR, D))
        mlp_b = lax.optimization_barrier(mlp_parts.astype(jnp.bfloat16))
        mlp_out = lax.optimization_barrier(jnp.sum(mlp_b.astype(jnp.float32), axis=0))
        output = (middle + mlp_out).astype(jnp.bfloat16)
        d_swiglu = contract('pd,fd->pf', cotangent, down_proj)
        grad_down = contract('pf,pd->fd', swiglu, cotangent)
        gate_sig = jax.nn.sigmoid(gate_pre)
        d_gate = d_swiglu * up_pre * gate_sig * (1.0 + gate_pre * (1.0 - gate_sig))
        d_up = d_swiglu * gate_pre * gate_sig
        d_gate_up = jnp.stack([d_gate, d_up], axis=1).astype(jnp.bfloat16)
        grad_gu = contract('pd,pkf->dkf', normed_two, d_gate_up)
        d_normed_two = contract('pkf,dkf->pd', d_gate_up, gate_up)
        d_middle_norm, grad_mlp = rms_backward(middle, scale_two, mlp_gain, d_normed_two)
        d_middle = cotangent.astype(jnp.float32) + d_middle_norm
        d_branch = d_middle.astype(jnp.bfloat16)
        d_attended = contract('pd,cd->pc', d_branch, o_proj).astype(jnp.bfloat16)
        grad_o = contract('pc,pd->cd', attended_flat, d_branch)
        d_heads = d_attended.reshape(LEN, AH, HD)
        d_values = contract('hpk,phc->khc', probs_b, d_heads)
        d_probs = contract('phc,khc->hpk', d_heads, value_heads)
        d_scores = (attn_probs * (d_probs - lax.optimization_barrier(jnp.sum(attn_probs * d_probs, axis=-1, keepdims=True))) * score_scale).astype(jnp.bfloat16)
        d_queries = contract('hpk,khc->phc', d_scores, key_heads)
        d_keys = contract('hpk,phc->khc', d_scores, queries)
        key_blocks = lax.optimization_barrier(jnp.sum(d_keys.reshape(LEN, N_TENSOR, heads_dev, HD), axis=2))
        value_blocks = lax.optimization_barrier(jnp.sum(d_values.reshape(LEN, N_TENSOR, heads_dev, HD), axis=2))
        query_grad_b = rotate(d_queries, cosine, sine_tab, -1.0).astype(jnp.bfloat16).reshape(LEN, AH * HD)
        kv_grad_b = jnp.stack([rotate(key_blocks, cosine, sine_tab, -1.0), value_blocks], axis=2).astype(jnp.bfloat16)
        grad_q = contract('pd,pc->dc', normed, query_grad_b)
        grad_kv = jnp.einsum('pd,pjkc,jh->dhkc', normed.astype(jnp.float32), kv_grad_b.astype(jnp.float32), select)
        d_normed = contract('pc,dc->pd', query_grad_b, q_proj)
        d_normed = d_normed + jnp.einsum('pjkc,jh,dhkc->pd', kv_grad_b.astype(jnp.float32), select, kv_proj.astype(jnp.float32))
        d_mamba_y = contract('pd,cd->pc', d_branch, out_proj)
        grad_out = contract('pc,pd->cd', mamba_y, d_branch)
        d_zx, d_bc_rep, d_raw, g_conv_w, g_conv_b, g_rate, g_shift, g_skip, g_gate = mamba_pull(d_mamba_y)
        d_zx_b = d_zx.astype(jnp.bfloat16)
        d_bc_b = d_bc_rep.astype(jnp.bfloat16)
        d_raw_b = d_raw.astype(jnp.bfloat16)
        grad_zx = contract('pd,pkc->dkc', normed, d_zx_b)
        grad_bc = contract('pd,jpn->dn', normed, d_bc_b)
        grad_dt = contract('pd,ph->dh', normed, d_raw_b)
        d_normed = d_normed + contract('pkc,dkc->pd', d_zx_b, in_proj) + contract('jpn,dn->pd', d_bc_b, bc_proj) + contract('ph,dh->pd', d_raw_b, step_proj)
        d_inputs_norm, grad_norm = rms_backward(inputs32, scale_one, norm_gain, d_normed)
        d_hid = d_middle + d_inputs_norm
        grads = (grad_norm, grad_mlp, grad_zx, grad_dt, grad_bc, grad_out, grad_q, grad_kv, grad_o, grad_gu, grad_down, g_conv_w, g_conv_b, g_rate, g_shift, g_skip, g_gate)
        new_sums = tuple((left + right for left, right in zip(grad_sums, grads)))
        return (new_sums, (output, d_hid))
    sums_out, (outputs, d_hiddens) = lax.scan(one_sequence, zero_sums, (hidden, out_grad))
    return (outputs, d_hiddens, sums_out[0], sums_out[1], sums_out[2], sums_out[3], sums_out[4], sums_out[5], sums_out[6], sums_out[7], sums_out[8], sums_out[9], sums_out[10], sums_out[11], sums_out[12], sums_out[13], sums_out[14], sums_out[15], sums_out[16])
```

```python
import math

import jax
import jax.numpy as jnp
from jax import lax
from jax.experimental import pallas as pl
from jax.experimental.pallas import tpu as pltpu
from jax.sharding import PartitionSpec as P

AH = 8
KVH = 2
GN_GROUP = 384

EPS = 1e-05
ROPE_BASE = 100000000000.0
HIGHEST = lax.Precision.HIGHEST
F32 = jnp.float32
BF16 = jnp.bfloat16
LANES = 128
PAD = 8


def swap(value, axis, mask):
    count = lax.axis_size(axis)
    return lax.ppermute(value, axis, [(i, i ^ mask) for i in range(count)])


def fast_plane():
    return lax.axis_size("shard") == 2 and lax.axis_size("ctx") == 4


def block_orders():
    shard, ctx = lax.axis_index("shard"), lax.axis_index("ctx")
    count = lax.axis_size("shard") * lax.axis_size("ctx")
    if not fast_plane():
        return None, None, count
    here = shard * 4 + ctx
    offsets = [dx * 4 + dy * 2 + dc for dc in (0, 1) for dx in (0, 1) for dy in (0, 1)]
    held = [here ^ off for off in offsets]
    back = []
    for block in range(count):
        off = here ^ block
        back.append((off & 1) * 4 + (off >> 2) * 2 + ((off >> 1) & 1))
    return held, back, count


def reorder(value, order, count):
    if order is None:
        return value
    width = value.shape[-1] // count
    return jnp.concatenate(
        [lax.dynamic_slice_in_dim(value, at * width, width, value.ndim - 1) for at in order], axis=-1
    )


def plane_gather(piece):
    if not fast_plane():
        return lax.all_gather(piece, ("shard", "ctx"), axis=0, tiled=True)
    half = piece.shape[0] // 2
    over_x = swap(piece, "shard", 1)
    over_y = swap(piece, "ctx", 2)
    other_own = swap(piece, "ctx", 1)
    diag_a = swap(over_x[:half], "ctx", 2)
    diag_b = swap(over_y[half:], "shard", 1)
    other_y = swap(over_y, "ctx", 1)
    other_x = swap(over_x, "ctx", 1)
    diag = jnp.concatenate([diag_a, diag_b], axis=0)
    other_diag = swap(diag, "ctx", 1)
    return jnp.concatenate(
        [piece, over_y, over_x, diag, other_own, other_y, other_x, other_diag], axis=0
    )


def add16(left, right):
    return (left.astype(F32) + right.astype(F32)).astype(BF16)


def plane_scatter(grads):
    if not fast_plane():
        return lax.psum_scatter(grads, ("shard", "ctx"), scatter_dimension=0, tiled=True)
    rows = grads.shape[0] // 8
    cols = (grads.shape[1] // (2 * LANES)) * LANES
    got = swap(grads[4 * rows :], "ctx", 1)
    kept = add16(grads[: 4 * rows], got)
    left, right = kept[:, :cols], kept[:, cols:]
    got_left = swap(left[2 * rows :], "shard", 1)
    send_right = jnp.concatenate([right[rows : 2 * rows], right[3 * rows :]], axis=0)
    got_right = swap(send_right, "ctx", 2)
    left = add16(left[: 2 * rows], got_left)
    right = add16(jnp.concatenate([right[:rows], right[2 * rows : 3 * rows]], axis=0), got_right)
    last_left = swap(left[rows:], "ctx", 2)
    last_right = swap(right[rows:], "shard", 1)
    return jnp.concatenate(
        [
            left[:rows].astype(F32) + last_left.astype(F32),
            right[:rows].astype(F32) + last_right.astype(F32),
        ],
        axis=1,
    )


def pair_tables(count):
    first = [(src, dst) for dst, src in ((0, 1), (1, 2), (2, 0))]
    second = [(src, dst) for dst, src in ((1, 3), (2, 1), (3, 2))]
    assert count == 4
    return first, second


def half_gather(piece, tau):
    first, second = pair_tables(lax.axis_size("tensor"))
    got_a = lax.ppermute(piece, "tensor", first)
    got_b = lax.ppermute(piece, "tensor", second)
    low = jnp.where(tau == 0, piece, jnp.where(tau == 3, got_b, got_a))
    high = jnp.where(tau == 0, got_a, jnp.where(tau == 3, piece, got_b))
    return low, high


def half_scatter(low, high, tau):
    first, second = pair_tables(lax.axis_size("tensor"))
    low16, high16 = low.astype(BF16), high.astype(BF16)
    got_a = lax.ppermute(jnp.where(tau == 0, high16, low16), "tensor", [(b, a) for a, b in first])
    got_b = lax.ppermute(jnp.where(tau == 3, low16, high16), "tensor", [(b, a) for a, b in second])
    own = jnp.where(tau == 0, low, jnp.where(tau == 3, high, 0.0))
    return own + got_a.astype(F32) + got_b.astype(F32)


def pair_sum(part):
    own = part.astype(BF16)
    return own.astype(F32) + swap(own, "tensor", 1).astype(F32)


def total(value):
    for axis in ("ctx", "shard", "tensor"):
        mask = 1
        while mask < lax.axis_size(axis):
            value = value + swap(value, axis, mask)
            mask *= 2
    return value


def call(body, outs, *args):
    return pl.pallas_call(
        body,
        out_shape=tuple(jax.ShapeDtypeStruct(shape, kind) for shape, kind in outs),
        compiler_params=pltpu.CompilerParams(vmem_limit_bytes=56 * 1024 * 1024),
    )(*args)


def mm(left, right, dims=((1,), (0,))):
    return lax.dot_general(
        left.astype(BF16), right.astype(BF16), (dims, ((), ())), preferred_element_type=F32
    )


def mm32(left, right):
    return lax.dot_general(
        left, right, (((1,), (0,)), ((), ())), precision=HIGHEST, preferred_element_type=F32
    )


def widen(values, heads, rows, width):
    lane = lax.broadcasted_iota(jnp.int32, (rows, 2 * width), 1)
    parts = []
    for head in range(0, heads, 2):
        even = jnp.broadcast_to(values[:, head : head + 1], (rows, 2 * width))
        odd = jnp.broadcast_to(values[:, head + 1 : head + 2], (rows, 2 * width))
        parts.append(jnp.where(lane < width, even, odd))
    return jnp.concatenate(parts, axis=1)


def narrow(values, heads, rows, width):
    lane = lax.broadcasted_iota(jnp.int32, (rows, 2 * width), 1)
    at = lax.broadcasted_iota(jnp.int32, (rows, LANES), 1)
    out = jnp.zeros((rows, LANES), F32)
    for head in range(0, heads, 2):
        pair = values[:, head * width : (head + 2) * width]
        whole = jnp.sum(pair, axis=1, keepdims=True)
        even = jnp.sum(jnp.where(lane < width, pair, 0.0), axis=1, keepdims=True)
        out = jnp.where(at == head, even, out)
        out = jnp.where(at == head + 1, whole - even, out)
    return out


def narrow_exact(values, heads, rows, width):
    lane = lax.broadcasted_iota(jnp.int32, (rows, 2 * width), 1)
    at = lax.broadcasted_iota(jnp.int32, (rows, LANES), 1)
    out = jnp.zeros((rows, LANES), F32)
    for head in range(0, heads, 2):
        pair = values[:, head * width : (head + 2) * width]
        even = jnp.sum(jnp.where(lane < width, pair, 0.0), axis=1, keepdims=True)
        odd = jnp.sum(jnp.where(lane < width, 0.0, pair), axis=1, keepdims=True)
        out = jnp.where(at == head, even, out)
        out = jnp.where(at == head + 1, odd, out)
    return out


def sigmoid(value):
    return jax.nn.sigmoid(value)


def turn(values, cosine, sine):
    half = values.shape[1] // 2
    first, second = values[:, :half], values[:, half:]
    return jnp.concatenate([first * cosine - second * sine, second * cosine + first * sine], axis=1)


def triangle(rows, lower):
    row = lax.broadcasted_iota(jnp.int32, (rows, rows), 0)
    col = lax.broadcasted_iota(jnp.int32, (rows, rows), 1)
    return row >= col if lower else row <= col


def conv_pre(pre_ref, cw_ref, cb_ref, rows, width, lags):
    out = cb_ref[0:1, :]
    for lag in range(lags):
        start = PAD - (lags - 1) + lag
        out = out + cw_ref[lag : lag + 1, :] * pre_ref[start : start + rows, 0:width]
    return out


def per_device(
    hidden,
    out_grad,
    norm_gain,
    mlp_gain,
    in_proj,
    step_proj,
    bc_proj,
    out_proj,
    q_proj,
    kv_proj,
    o_proj,
    gate_up,
    down_proj,
    conv_weight,
    conv_bias,
    log_rate,
    step_bias,
    skip_gain,
    gate_gain,
):
    tau = lax.axis_index("tensor")
    rank = tau % 2
    group = tau // 2
    ctx = lax.axis_index("ctx")
    n_ctx = lax.axis_size("ctx")
    n_tensor = lax.axis_size("tensor")
    assert n_tensor == 4 and hidden.shape[0] == 2
    rows, width = hidden.shape[1:]
    own_rows = in_proj.shape[0]
    chan_q = in_proj.shape[2]
    chan = 2 * chan_q
    heads_q = step_proj.shape[1]
    heads = 2 * heads_q
    hdm = chan // heads
    nstate = bc_proj.shape[1] // 2
    act_w = chan + 2 * nstate
    lags = conv_weight.shape[0]
    d_inner = gate_gain.shape[0]
    hd = kv_proj.shape[3]
    q_q = q_proj.shape[1]
    q_w = 2 * q_q
    q_heads = q_w // hd
    ff_q = gate_up.shape[2]
    ff = 2 * ff_q
    kv_w = 2 * hd
    kv_head = rank * q_heads // (AH // KVH)
    scale = 1.0 / math.sqrt(hd)
    ext = rows + PAD
    n_groups = chan // GN_GROUP
    pairs = heads // 2
    pair_w = 2 * hdm

    held, back, blocks = block_orders()

    own_hidden = lax.dynamic_index_in_dim(hidden, group, 0, keepdims=False)
    own_cot = lax.dynamic_index_in_dim(out_grad, group, 0, keepdims=False)
    halo = lax.ppermute(
        own_hidden[rows - PAD :], "ctx", [(i, i + 1) for i in range(n_ctx - 1)]
    )
    pad_row = lax.broadcasted_iota(jnp.int32, (PAD, 1), 0)
    halo = jnp.where(pad_row >= PAD - (lags - 1), halo, jnp.zeros_like(halo))

    quarter_a = jnp.concatenate(
        [
            in_proj[:, 1],
            in_proj[:, 0],
            q_proj,
            jnp.pad(step_proj, ((0, 0), (0, LANES - heads_q))),
        ],
        axis=1,
    )
    low_a, high_a = half_gather(quarter_a, tau)
    own_kv = lax.dynamic_index_in_dim(kv_proj, kv_head, 1, keepdims=False).reshape(own_rows, kv_w)
    cut = 2 * chan_q
    step_at = cut + q_q
    piece_a = jnp.concatenate(
        [
            low_a[:, :chan_q],
            high_a[:, :chan_q],
            bc_proj,
            low_a[:, chan_q:cut],
            high_a[:, chan_q:cut],
            low_a[:, cut:step_at],
            high_a[:, cut:step_at],
            own_kv,
            jnp.concatenate(
                [
                    low_a[:, step_at : step_at + heads_q],
                    high_a[:, step_at : step_at + heads_q],
                    jnp.zeros((own_rows, LANES - heads), BF16),
                ],
                axis=1,
            ),
        ],
        axis=1,
    )
    at_z = act_w
    at_q = at_z + chan
    at_kv = at_q + q_w
    at_step = at_kv + kv_w
    wide_a = plane_gather(piece_a)

    quarter_b = jnp.concatenate(
        [out_proj.T, o_proj.T, gate_up[:, 0], gate_up[:, 1], down_proj.T], axis=1
    )
    quarter_b, _ = lax.optimization_barrier((quarter_b, low_a))
    low_b, high_b = half_gather(quarter_b, tau)
    cuts = [0, chan_q, chan_q + q_q]
    for _ in range(3):
        cuts.append(cuts[-1] + ff_q)
    piece_b = jnp.concatenate(
        [part[:, lo:hi] for lo, hi in zip(cuts[:-1], cuts[1:]) for part in (low_b, high_b)], axis=1
    )
    wide_b = plane_gather(piece_b)
    mix_w = chan + q_w
    w_mix = wide_b[:, :mix_w]
    w_gu = wide_b[:, mix_w : mix_w + 2 * ff]
    w_down = wide_b[:, mix_w + 2 * ff :]

    chan_at = rank * chan
    conv_w = jnp.concatenate(
        [lax.dynamic_slice_in_dim(conv_weight, chan_at, chan, 1), conv_weight[:, d_inner:]], axis=1
    )
    conv_w = jnp.pad(conv_w, ((0, 8 - lags), (0, 0)))
    conv_b = jnp.concatenate(
        [lax.dynamic_slice_in_dim(conv_bias, chan_at, chan, 0), conv_bias[d_inner:]], axis=0
    )[None]
    head_at = rank * heads
    head_vec = jnp.stack(
        [
            jnp.pad(lax.dynamic_slice_in_dim(vec, head_at, heads, 0), (0, LANES - heads))
            for vec in (log_rate, step_bias, skip_gain)
        ]
    )
    head_vec = jnp.pad(head_vec, ((0, 5), (0, 0)))
    gate_g = lax.dynamic_slice_in_dim(gate_gain, chan_at, chan, 0)[None]
    positions = (ctx * rows + jnp.arange(rows, dtype=jnp.int32)).astype(F32)
    inv_freq = jnp.exp(jnp.arange(hd // 2, dtype=F32) * (-2.0 * math.log(ROPE_BASE) / hd))
    angle = positions[:, None] * inv_freq[None, :]
    cosine, sine = jnp.cos(angle), jnp.sin(angle)

    gain_one = reorder(norm_gain[None], held, blocks)
    gain_two = reorder(mlp_gain[None], held, blocks)
    ext16 = reorder(jnp.concatenate([halo, own_hidden], axis=0), held, blocks)
    cot16 = reorder(own_cot, held, blocks)
    ext32 = ext16.astype(F32)
    scale_ext = lax.rsqrt(jnp.mean(ext32 * ext32, axis=1, keepdims=True) + EPS)
    normed = (ext32 * scale_ext * gain_one).astype(BF16)
    inputs32 = ext32[PAD:]
    scale_one = scale_ext[PAD:]
    pre = mm(normed, wide_a)

    def split_body(pre_ref, cw_ref, cb_ref, hv_ref, cos_ref, sin_ref, act_ref, dtc_ref, st_ref, q_ref, kv_ref):
        value = conv_pre(pre_ref, cw_ref, cb_ref, rows, act_w, lags)
        act = (value * sigmoid(value)).astype(BF16)
        act_ref[...] = act
        lane = lax.broadcasted_iota(jnp.int32, (rows, LANES), 1)
        raw = pre_ref[PAD:ext, at_step : at_step + LANES] + hv_ref[1:2, :]
        dt = jnp.maximum(raw, 0.0) + jnp.log1p(jnp.exp(-jnp.abs(raw)))
        dt = jnp.where(lane < heads, dt, 0.0)
        rate = -jnp.exp(hv_ref[0:1, :])
        cum = mm32(triangle(rows, True).astype(F32), dt * rate)
        dtc_ref[:, :LANES] = dt
        dtc_ref[:, LANES:] = cum
        last = cum[rows - 1 : rows]
        factor = widen(jnp.exp(last - cum) * dt, heads, rows, hdm)
        scaled = (act[:, :chan].astype(F32) * factor).astype(BF16)
        b_mat = act[:, chan : chan + nstate]
        st_ref[0:nstate, :] = mm(b_mat, scaled, ((0,), (0,))).astype(BF16)
        decay = widen(jnp.exp(cum[rows - 8 : rows]), heads, 8, hdm)
        st_ref[nstate:, :] = jnp.broadcast_to(decay[7:8], (16, chan)).astype(BF16)
        cosv, sinv = cos_ref[...], sin_ref[...]
        for head in range(q_heads):
            part = pre_ref[PAD:ext, at_q + head * hd : at_q + (head + 1) * hd]
            q_ref[:, head * hd : (head + 1) * hd] = turn(part, cosv, sinv).astype(BF16)
        kv_ref[:, :hd] = turn(pre_ref[PAD:ext, at_kv : at_kv + hd], cosv, sinv).astype(BF16)
        kv_ref[:, hd:] = pre_ref[PAD:ext, at_kv + hd : at_kv + kv_w].astype(BF16)

    act, dtc, st_own, query, kv_own = call(
        split_body,
        [
            ((rows, act_w), BF16),
            ((rows, 2 * LANES), F32),
            ((nstate + 16, chan), BF16),
            ((rows, q_w), BF16),
            ((rows, kv_w), BF16),
        ],
        pre, conv_w, conv_b, head_vec, cosine, sine,
    )
    kv_all = [kv_own] + [swap(kv_own, "ctx", k) for k in range(1, n_ctx)]
    st_all = [swap(st_own, "ctx", k) for k in range(1, n_ctx)]
    ids = [ctx ^ k for k in range(1, n_ctx)]

    def local_body(act_ref, dtc_ref, hv_ref, y_ref):
        b_mat = act_ref[:, chan : chan + nstate]
        c_mat = act_ref[:, chan + nstate :]
        inner = mm(c_mat, b_mat, ((1,), (1,)))
        dt_t = dtc_ref[:, :LANES].T
        cum = dtc_ref[:, LANES:]
        cum_t = cum.T
        below = triangle(rows, True)
        lane = lax.broadcasted_iota(jnp.int32, (rows, pair_w), 1)
        skip = widen(jnp.broadcast_to(hv_ref[2:3, :], (8, LANES)), heads, 8, hdm)[0:1]
        for pair in range(pairs):
            x_pair = act_ref[:, pair * pair_w : (pair + 1) * pair_w]
            halves = []
            for head in (2 * pair, 2 * pair + 1):
                gap = cum[:, head : head + 1] - cum_t[head : head + 1, :]
                kern = jnp.exp(jnp.where(below, gap, -1e30)) * inner * dt_t[head : head + 1, :]
                halves.append(mm(kern, x_pair))
            y_ref[:, pair * pair_w : (pair + 1) * pair_w] = (
                jnp.where(lane < hdm, halves[0], halves[1])
                + skip[:, pair * pair_w : (pair + 1) * pair_w] * x_pair.astype(F32)
            )

    (y_local,) = call(local_body, [((rows, chan), F32)], act, dtc, head_vec)

    ctx_word = jnp.full((1,), ctx, jnp.int32)

    def attend_body(ctx_ref, q_ref, *refs):
        kv_refs, (o_ref, lse_ref) = refs[:n_ctx], refs[n_ctx:]
        q = q_ref[...]
        scores = []
        for k in range(n_ctx):
            part = mm(q, kv_refs[k][:, :hd], ((1,), (1,))) * scale
            if k == 0:
                part = jnp.where(triangle(rows, True), part, -1e30)
            else:
                part = jnp.where((ctx_ref[0] ^ k) < ctx_ref[0], part, -1e30)
            scores.append(part)
        peak = scores[0].max(axis=1, keepdims=True)
        for part in scores[1:]:
            peak = jnp.maximum(peak, part.max(axis=1, keepdims=True))
        probs = [jnp.exp(part - peak) for part in scores]
        norm = probs[0].sum(axis=1, keepdims=True)
        for part in probs[1:]:
            norm = norm + part.sum(axis=1, keepdims=True)
        inverse = 1.0 / norm
        out = jnp.zeros((rows, hd), F32)
        for k in range(n_ctx):
            out = out + mm(probs[k] * inverse, kv_refs[k][:, hd:])
        o_ref[...] = out.astype(BF16)
        lse_ref[...] = jnp.broadcast_to(peak + jnp.log(norm), (rows, LANES))

    whole_kv = pl.BlockSpec((rows, kv_w), lambda h, c: (0, 0))
    per_head = pl.BlockSpec((rows, hd), lambda h, c: (0, h))
    lse_spec = pl.BlockSpec((rows, LANES), lambda h, c: (0, h))
    attended, lse = pl.pallas_call(
        attend_body,
        grid_spec=pltpu.PrefetchScalarGridSpec(
            num_scalar_prefetch=1,
            grid=(q_heads,),
            in_specs=[per_head] + [whole_kv] * n_ctx,
            out_specs=(per_head, lse_spec),
        ),
        out_shape=(
            jax.ShapeDtypeStruct((rows, q_w), BF16),
            jax.ShapeDtypeStruct((rows, q_heads * LANES), F32),
        ),
        compiler_params=pltpu.CompilerParams(vmem_limit_bytes=56 * 1024 * 1024),
    )(ctx_word, query, *kv_all)

    decays = [part[nstate : nstate + 1].astype(F32) for part in st_all]
    state_in = jnp.zeros((nstate, chan), F32)
    for k, part in enumerate(st_all):
        weight = jnp.where(ids[k] < ctx, 1.0, 0.0)
        for m, decay in enumerate(decays):
            if m != k:
                weight = weight * jnp.where((ids[k] < ids[m]) & (ids[m] < ctx), decay, 1.0)
        state_in = state_in + weight * part[:nstate].astype(F32)

    def gate_body(pre_ref, act_ref, dtc_ref, y_ref, s_ref, g_ref, out_ref, ym_ref):
        c_mat = act_ref[:, chan + nstate :]
        carried = mm(c_mat, s_ref[...])
        y_all = y_ref[...] + carried * widen(jnp.exp(dtc_ref[:, LANES:]), heads, rows, hdm)
        out_ref[...] = y_all
        z = pre_ref[PAD:ext, at_z : at_z + chan]
        gated = y_all * (z * sigmoid(z))
        for grp in range(n_groups):
            part = gated[:, grp * GN_GROUP : (grp + 1) * GN_GROUP]
            inv = lax.rsqrt(jnp.mean(part * part, axis=1, keepdims=True) + EPS)
            gain = g_ref[0:1, grp * GN_GROUP : (grp + 1) * GN_GROUP]
            ym_ref[:, grp * GN_GROUP : (grp + 1) * GN_GROUP] = (part * inv * gain).astype(BF16)

    y_all, mamba_y = call(
        gate_body,
        [((rows, chan), F32), ((rows, chan), BF16)],
        pre, act, dtc, y_local, state_in, gate_g,
    )

    mixed_in = jnp.concatenate([mamba_y, attended], axis=1)
    mixed = pair_sum(mm(mixed_in, w_mix, ((1,), (1,))))
    middle = inputs32 + mixed
    scale_two = lax.rsqrt(jnp.mean(middle * middle, axis=1, keepdims=True) + EPS)
    normed_two = (middle * scale_two * gain_two).astype(BF16)

    gate_up32 = mm(normed_two, w_gu)
    gate_pre, up_pre = gate_up32[:, :ff], gate_up32[:, ff:]
    gate_sig = sigmoid(gate_pre)
    swiglu = (gate_pre * gate_sig * up_pre).astype(BF16)
    d_swiglu = mm(cot16, w_down)
    d_gate = d_swiglu * up_pre * gate_sig * (1.0 + gate_pre * (1.0 - gate_sig))
    d_up = d_swiglu * gate_pre * gate_sig
    d_gate_up = jnp.concatenate([d_gate.astype(BF16), d_up.astype(BF16)], axis=1)
    d_normed_two = pair_sum(mm(d_gate_up, w_gu, ((1,), (1,))))
    mlp_out = pair_sum(mm(swiglu, w_down, ((1,), (1,))))
    out_own = (middle + mlp_out).astype(BF16)
    out_other = swap(out_own, "tensor", 2)

    def ordered(own, other):
        pair = jnp.where(group == 0, jnp.stack([own, other]), jnp.stack([other, own]))
        return reorder(pair, back, blocks)

    output = ordered(out_own, out_other)

    weighted = d_normed_two * gain_two
    inner_mean = jnp.mean(weighted * middle, axis=1, keepdims=True)
    d_middle = cot16.astype(F32) + scale_two * (
        weighted - middle * scale_two * scale_two * inner_mean
    )
    grad_mlp = jnp.sum(d_normed_two * middle * scale_two, axis=0)
    d_branch = d_middle.astype(BF16)

    d_mixed = mm(d_branch, w_mix)
    d_att = d_mixed[:, chan:].astype(BF16)
    d_mamba = d_mixed[:, :chan]

    def gate_back(pre_ref, act_ref, dtc_ref, y_ref, d_ref, g_ref, dy_ref, dz_ref, gs_ref, gg_ref):
        c_mat = act_ref[:, chan + nstate :]
        grown = widen(jnp.exp(dtc_ref[:, LANES:]), heads, rows, hdm)
        dz_ref[0:PAD, :] = jnp.zeros((PAD, chan), BF16)
        for grp in range(n_groups):
            at = slice(grp * GN_GROUP, (grp + 1) * GN_GROUP)
            z = pre_ref[PAD:ext, at_z + grp * GN_GROUP : at_z + (grp + 1) * GN_GROUP]
            sig = sigmoid(z)
            silu = z * sig
            y = y_ref[:, at]
            gated = y * silu
            inv = lax.rsqrt(jnp.mean(gated * gated, axis=1, keepdims=True) + EPS)
            unit = gated * inv
            d_out = d_ref[:, at]
            gg_ref[:, at] = jnp.broadcast_to(jnp.sum(d_out * unit, axis=0, keepdims=True), (8, GN_GROUP))
            w = d_out * g_ref[0:1, at]
            d_gated = inv * (w - unit * jnp.mean(w * unit, axis=1, keepdims=True))
            dy_ref[:, at] = d_gated * silu
            dz_ref[PAD:ext, at] = (d_gated * y * (sig * (1.0 + z * (1.0 - sig)))).astype(BF16)
        gs_ref[...] = mm(c_mat, dy_ref[...] * grown, ((0,), (0,))).astype(BF16)

    d_y, d_z, gs_own, grad_gate = call(
        gate_back,
        [((rows, chan), F32), ((ext, chan), BF16), ((nstate, chan), BF16), ((8, chan), F32)],
        pre, act, dtc, y_all, d_mamba, gate_g,
    )
    gs_all = [swap(gs_own, "ctx", k) for k in range(1, n_ctx)]

    def attend_back(ctx_ref, q_ref, do_ref, lse_ref, cos_ref, sin_ref, *refs):
        kv_refs, dq_ref = refs[:n_ctx], refs[n_ctx]
        out_refs, acc_ref = refs[n_ctx + 1 : 2 * n_ctx + 1], refs[2 * n_ctx + 1]
        head = pl.program_id(0)

        @pl.when(head == 0)
        def _():
            acc_ref[...] = jnp.zeros_like(acc_ref)

        q = q_ref[...]
        d_o = do_ref[...]
        lse = lse_ref[:, 0:1]
        probs, d_probs = [], []
        dot = jnp.zeros((rows, 1), F32)
        for k in range(n_ctx):
            part = mm(q, kv_refs[k][:, :hd], ((1,), (1,))) * scale
            if k == 0:
                part = jnp.where(triangle(rows, True), part, -1e30)
            else:
                part = jnp.where((ctx_ref[0] ^ k) < ctx_ref[0], part, -1e30)
            part = jnp.exp(part - lse)
            d_part = mm(d_o, kv_refs[k][:, hd:], ((1,), (1,)))
            dot = dot + jnp.sum(part * d_part, axis=1, keepdims=True)
            probs.append(part)
            d_probs.append(d_part)
        d_q = jnp.zeros((rows, hd), F32)
        for k in range(n_ctx):
            d_s = (probs[k] * (d_probs[k] - dot) * scale).astype(BF16)
            d_q = d_q + mm(d_s, kv_refs[k][:, :hd])
            acc_ref[k * rows : (k + 1) * rows, :hd] += mm(d_s, q, ((0,), (0,)))
            acc_ref[k * rows : (k + 1) * rows, hd:] += mm(probs[k], d_o, ((0,), (0,)))
        dq_ref[0:PAD, :] = jnp.zeros((PAD, hd), BF16)
        dq_ref[PAD:, :] = turn(d_q, cos_ref[...], -sin_ref[...]).astype(BF16)

        @pl.when(head == q_heads - 1)
        def _():
            for k in range(n_ctx):
                out_refs[k][...] = acc_ref[k * rows : (k + 1) * rows, :].astype(BF16)

    table = pl.BlockSpec((rows, hd // 2), lambda h, c: (0, 0))
    back_out = pl.pallas_call(
        attend_back,
        grid_spec=pltpu.PrefetchScalarGridSpec(
            num_scalar_prefetch=1,
            grid=(q_heads,),
            in_specs=[per_head, per_head, lse_spec, table, table] + [whole_kv] * n_ctx,
            out_specs=tuple([pl.BlockSpec((ext, hd), lambda h, c: (0, h))] + [whole_kv] * n_ctx),
            scratch_shapes=[pltpu.VMEM((n_ctx * rows, kv_w), F32)],
        ),
        out_shape=tuple(
            [jax.ShapeDtypeStruct((ext, q_w), BF16)]
            + [jax.ShapeDtypeStruct((rows, kv_w), BF16)] * n_ctx
        ),
        compiler_params=pltpu.CompilerParams(vmem_limit_bytes=56 * 1024 * 1024),
    )(ctx_word, query, d_att, lse, cosine, sine, *kv_all)
    d_q = back_out[0]
    d_kv32 = back_out[1].astype(F32)
    for k in range(1, n_ctx):
        d_kv32 = d_kv32 + swap(back_out[1 + k], "ctx", k).astype(F32)
    d_kv = jnp.concatenate([turn(d_kv32[:, :hd], cosine, -sine), d_kv32[:, hd:]], axis=1).astype(BF16)
    d_kv = jnp.pad(d_kv, ((PAD, 0), (0, 0)))

    d_state = jnp.zeros((nstate, chan), F32)
    for k, part in enumerate(gs_all):
        weight = jnp.where(ids[k] > ctx, 1.0, 0.0)
        for m, decay in enumerate(decays):
            if m != k:
                weight = weight * jnp.where((ids[k] > ids[m]) & (ids[m] > ctx), decay, 1.0)
        d_state = d_state + weight * part.astype(F32)

    def scan_back(
        pre_ref, act_ref, dtc_ref, dy_ref, s_ref, ds_ref, cw_ref, cb_ref, hv_ref,
        dx_ref, dr_ref, gc_ref, gh_ref, tall_ref,
    ):
        b_mat = act_ref[:, chan : chan + nstate]
        c_mat = act_ref[:, chan + nstate : act_w]
        dt = dtc_ref[:, :LANES]
        cum = dtc_ref[:, LANES:]
        dt_t, cum_t = dt.T, cum.T
        last = cum[rows - 1 : rows]
        tail = jnp.exp(last - cum)
        factor = tail * dt
        below = triangle(rows, True)
        lane = lax.broadcasted_iota(jnp.int32, (rows, pair_w), 1)
        at_head = lax.broadcasted_iota(jnp.int32, (rows, LANES), 1)
        inner = mm(c_mat, b_mat, ((1,), (1,)))
        x32 = act_ref[:, :chan].astype(F32)
        d_y = dy_ref[...]
        grown = d_y * widen(jnp.exp(cum), heads, rows, hdm)
        s_in = s_ref[...]
        d_so = ds_ref[...]
        d_c = mm(grown, s_in, ((1,), (1,)))
        d_cum = narrow_exact(grown * mm(c_mat, s_in), heads, rows, hdm)
        v = mm(b_mat, d_so)
        wide_f = widen(factor, heads, rows, hdm)
        d_b = mm(x32 * wide_f, d_so, ((1,), (1,)))
        d_f = narrow_exact(x32 * v, heads, rows, hdm)
        ends = jnp.broadcast_to(jnp.sum(d_so * s_in, axis=0, keepdims=True), (8, chan))
        end_h = narrow_exact(ends, heads, 8, hdm)[0:1] * jnp.exp(last)
        d_last = end_h + jnp.sum(d_f * factor, axis=0, keepdims=True)
        skips = jnp.broadcast_to(jnp.sum(d_y * x32, axis=0, keepdims=True), (8, chan))
        g_skip = narrow_exact(skips, heads, 8, hdm)[0:1]
        skip = widen(jnp.broadcast_to(hv_ref[2:3, :], (8, LANES)), heads, 8, hdm)[0:1]
        tall_ref[0:PAD, :] = jnp.zeros((PAD, act_w), F32)
        tall_ref[ext : ext + PAD, :] = jnp.zeros((PAD, act_w), F32)
        tall_ref[PAD:ext, :chan] = d_y * skip + v * wide_f
        d_inner_mat = jnp.zeros((rows, rows), F32)
        d_dt_rows = []
        d_y16 = d_y.astype(BF16)
        for pair in range(pairs):
            at = slice(pair * pair_w, (pair + 1) * pair_w)
            x_pair = act_ref[:, at]
            dy_pair = d_y16[:, at]
            halves = []
            for side in range(2):
                head = 2 * pair + side
                own = (lane < hdm) if side == 0 else (lane >= hdm)
                gap = cum[:, head : head + 1] - cum_t[head : head + 1, :]
                fall = jnp.exp(jnp.where(below, gap, -1e30))
                dt_row = dt_t[head : head + 1, :]
                d_kern = mm(jnp.where(own, dy_pair, jnp.zeros_like(dy_pair)), x_pair, ((1,), (1,)))
                d_fall = d_kern * fall
                d_inner_mat = d_inner_mat + d_fall * dt_row
                with_g = d_fall * inner
                d_dt_rows.append(jnp.sum(with_g, axis=0, keepdims=True))
                row_sum = jnp.sum(with_g * dt_row, axis=1, keepdims=True)
                d_cum = d_cum + jnp.where(at_head == head, row_sum, 0.0)
                halves.append(mm(fall * inner * dt_row, dy_pair, ((0,), (0,))))
            tall_ref[PAD:ext, at] += jnp.where(lane < hdm, halves[0], halves[1])
        fill = jnp.zeros((LANES - heads, rows), F32)
        d_dt_local = jnp.concatenate(d_dt_rows + [fill], axis=0).T
        tall_ref[PAD:ext, chan : chan + nstate] = d_b + mm(d_inner_mat, c_mat, ((0,), (0,)))
        tall_ref[PAD:ext, chan + nstate :] = d_c + mm(d_inner_mat, b_mat)
        row_at = lax.broadcasted_iota(jnp.int32, (rows, LANES), 0)
        d_cum = d_cum - dt * d_dt_local - d_f * factor + jnp.where(row_at == rows - 1, d_last, 0.0)
        back_sum = mm32(triangle(rows, False).astype(F32), d_cum)
        rate = -jnp.exp(hv_ref[0:1, :])
        d_dt = d_dt_local + d_f * tail + rate * back_sum
        g_rate = rate * jnp.sum(dt * back_sum, axis=0, keepdims=True)
        raw = pre_ref[PAD:ext, at_step : at_step + LANES] + hv_ref[1:2, :]
        d_raw = jnp.where(at_head < heads, d_dt * sigmoid(raw), 0.0)
        dr_ref[0:PAD, :] = jnp.zeros((PAD, LANES), BF16)
        dr_ref[PAD:, :] = d_raw.astype(BF16)
        gh_ref[...] = jnp.concatenate(
            [g_rate, jnp.sum(d_raw, axis=0, keepdims=True), g_skip, jnp.zeros((5, LANES), F32)], axis=0
        )
        value = conv_pre(pre_ref, cw_ref, cb_ref, rows, act_w, lags)
        sig = sigmoid(value)
        d_value = tall_ref[PAD:ext, :] * (sig * (1.0 + value * (1.0 - sig)))
        tall_ref[PAD:ext, :] = d_value
        sums = []
        out = jnp.zeros((ext, act_w), F32)
        for lag in range(lags):
            start = PAD - (lags - 1) + lag
            sums.append(jnp.sum(d_value * pre_ref[start : start + rows, 0:act_w], axis=0, keepdims=True))
            shift = lags - 1 - lag
            out = out + cw_ref[lag : lag + 1, :] * tall_ref[shift : shift + ext, :]
        sums.append(jnp.sum(d_value, axis=0, keepdims=True))
        sums.append(jnp.zeros((8 - len(sums), act_w), F32))
        gc_ref[...] = jnp.concatenate(sums, axis=0)
        dx_ref[...] = out.astype(BF16)

    d_xbc, d_raw, g_conv, g_head = pl.pallas_call(
        scan_back,
        out_shape=(
            jax.ShapeDtypeStruct((ext, act_w), BF16),
            jax.ShapeDtypeStruct((ext, LANES), BF16),
            jax.ShapeDtypeStruct((8, act_w), F32),
            jax.ShapeDtypeStruct((8, LANES), F32),
        ),
        scratch_shapes=[pltpu.VMEM((ext + PAD, act_w), F32)],
        compiler_params=pltpu.CompilerParams(vmem_limit_bytes=56 * 1024 * 1024),
    )(pre, act, dtc, d_y, state_in, d_state, conv_w, conv_b, head_vec)

    spill = lax.ppermute(d_xbc[:PAD], "ctx", [(i + 1, i) for i in range(n_ctx - 1)])
    tail_rows = add16(d_xbc[rows:], spill_rows(spill, lags))
    d_first = jnp.concatenate([d_xbc[PAD:rows], tail_rows], axis=0)
    rest = jnp.concatenate([d_z, d_q, d_kv, d_raw], axis=1)
    d_normed = mm(jnp.concatenate([d_first, rest[PAD:]], axis=1), wide_a, ((1,), (1,)))
    d_normed = pair_sum(d_normed)
    weighted = d_normed * gain_one
    inner_mean = jnp.mean(weighted * inputs32, axis=1, keepdims=True)
    d_hid = d_middle + scale_one * (weighted - inputs32 * scale_one * scale_one * inner_mean)
    grad_norm = jnp.sum(d_normed * inputs32 * scale_one, axis=0)
    d_hid = d_hid.astype(BF16)
    d_hidden = ordered(d_hid, swap(d_hid, "tensor", 2)).astype(F32)

    grad_b = jnp.concatenate(
        [
            mm(d_branch, mixed_in, ((0,), (0,))),
            mm(normed_two, d_gate_up, ((0,), (0,))),
            mm(cot16, swiglu, ((0,), (0,))),
        ],
        axis=1,
    ).astype(BF16)
    sum_b = plane_scatter(grad_b)
    low = [sum_b[:, 2 * lo : lo + hi] for lo, hi in zip(cuts[:-1], cuts[1:])]
    high = [sum_b[:, lo + hi : 2 * hi] for lo, hi in zip(cuts[:-1], cuts[1:])]
    mine_b = half_scatter(jnp.concatenate(low, axis=1), jnp.concatenate(high, axis=1), tau)
    grad_out = mine_b[:, : cuts[1]].T
    grad_o = mine_b[:, cuts[1] : cuts[2]].T
    grad_gu = jnp.stack([mine_b[:, cuts[2] : cuts[3]], mine_b[:, cuts[3] : cuts[4]]], axis=1)
    grad_down = mine_b[:, cuts[4] :].T

    d_all = jnp.concatenate([d_xbc, rest], axis=1)
    sum_a = plane_scatter(mm(normed, d_all, ((0,), (0,))).astype(BF16))

    def sides(at, size):
        return sum_a[:, at : at + size], sum_a[:, at + size : at + 2 * size]

    parts = [sides(0, chan_q), sides(at_z, chan_q), sides(at_q, q_q)]
    steps = sum_a[:, at_step : at_step + LANES]
    parts.append((steps, jnp.concatenate([steps[:, heads_q:], steps[:, :heads_q]], axis=1)))
    mine_a = half_scatter(
        jnp.concatenate([part[0] for part in parts], axis=1),
        jnp.concatenate([part[1] for part in parts], axis=1),
        tau,
    )
    grad_in = jnp.stack([mine_a[:, chan_q:cut], mine_a[:, :chan_q]], axis=1)
    grad_q = mine_a[:, cut:step_at]
    grad_step = mine_a[:, step_at : step_at + heads_q]

    shared = jnp.concatenate([sum_a[:, chan:at_z], sum_a[:, at_kv:at_step]], axis=1)
    thin = own_rows // n_tensor
    bc_w = 2 * nstate

    def chunk(k):
        return lax.dynamic_slice_in_dim(shared, (tau ^ k) * thin, thin, 0)

    shared16 = {k: swap(chunk(k).astype(BF16), "tensor", k).astype(F32) for k in range(1, n_tensor)}
    own_chunk = chunk(0)
    grad_bc = own_chunk[:, :bc_w] + sum(shared16[k][:, :bc_w] for k in range(1, n_tensor))
    same = own_chunk[:, bc_w:] + shared16[2][:, bc_w:]
    opposite = shared16[1][:, bc_w:] + shared16[3][:, bc_w:]
    grad_kv = jnp.stack(
        [jnp.where(rank == 0, same, opposite), jnp.where(rank == 0, opposite, same)], axis=1
    ).reshape(thin, KVH, 2, hd)

    once = (rank == 0).astype(F32)
    norms = reorder(jnp.stack([grad_norm, grad_mlp]) * once, back, blocks)
    full_conv = jnp.zeros((lags + 1, conv_weight.shape[1]), F32)
    full_conv = lax.dynamic_update_slice(full_conv, g_conv[: lags + 1, :chan], (0, chan_at))
    full_conv = lax.dynamic_update_slice(full_conv, g_conv[: lags + 1, chan:], (0, d_inner))
    full_head = lax.dynamic_update_slice(
        jnp.zeros((3, log_rate.shape[0]), F32), g_head[:3, :heads], (0, head_at)
    )
    full_gate = lax.dynamic_update_slice(jnp.zeros((d_inner,), F32), grad_gate[0], (chan_at,))
    pieces = [norms, full_conv, full_head, full_gate]
    flat = jnp.concatenate([piece.reshape(-1) for piece in pieces])
    size = flat.shape[0]
    flat = jnp.pad(flat, (0, -size % 1024)).reshape(-1, 128)
    flat = total(flat).reshape(-1)
    outs, at = [], 0
    for piece in pieces:
        outs.append(flat[at : at + piece.size].reshape(piece.shape))
        at += piece.size
    norms, full_conv, full_head, full_gate = outs
    return (
        output,
        d_hidden,
        norms[0],
        norms[1],
        grad_in,
        grad_step,
        grad_bc,
        grad_out,
        grad_q,
        grad_kv,
        grad_o,
        grad_gu,
        grad_down,
        full_conv[:lags],
        full_conv[lags],
        full_head[0],
        full_head[1],
        full_head[2],
        full_gate,
    )


def spill_rows(spill, lags):
    row = lax.broadcasted_iota(jnp.int32, (spill.shape[0], 1), 0)
    return jnp.where(row >= spill.shape[0] - (lags - 1), spill, jnp.zeros_like(spill))


def solution(mesh):
    wide = ("shard", "ctx")
    every = ("shard", "ctx", "tensor")
    return jax.shard_map(
        per_device,
        mesh=mesh,
        in_specs=(
            P("shard", "ctx", None),
            P("shard", "ctx", None),
            P(),
            P(),
            P(wide, None, "tensor"),
            P(wide, "tensor"),
            P(wide, None),
            P("tensor", wide),
            P(wide, "tensor"),
            P(wide, None, None, None),
            P("tensor", wide),
            P(wide, None, "tensor"),
            P("tensor", wide),
            P(),
            P(),
            P(),
            P(),
            P(),
            P(),
        ),
        out_specs=(
            P("shard", "ctx", None),
            P("shard", "ctx", None),
            P(),
            P(),
            P(wide, None, "tensor"),
            P(wide, "tensor"),
            P(every, None),
            P("tensor", wide),
            P(wide, "tensor"),
            P(every, None, None, None),
            P("tensor", wide),
            P(wide, None, "tensor"),
            P("tensor", wide),
            P(),
            P(),
            P(),
            P(),
            P(),
            P(),
        ),
        check_vma=False,
    )
```
